32 devices in a mesh: seq: 8 (over z, y), kvh: 4 (over x, core).
Axes of the slice: x: 2, y: 2, z: 4, core: 2. Of those that a mesh axis runs over, the one named last changes fastest.
Arguments:
- queries: bfloat16 [2048, 4096], P(('seq', 'kvh')), may hold values from -8 to 8
- keys: bfloat16 [2048, 2048], P(('seq', 'kvh')), may hold values from -8 to 8
- values: bfloat16 [2048, 2048], P(('seq', 'kvh')), may hold values from -6 to 6
- out_grad: bfloat16 [2048, 4096], P(('seq', 'kvh')), may hold values from -6 to 6
- file_start: int32 [2048], P('seq'), may hold values from 0 to 2047, as said below
Outputs:
- attn_out: bfloat16 [2048, 4096], P(('seq', 'kvh'))
- query_grad: bfloat16 [2048, 4096], P(('seq', 'kvh'))
- key_gradient: bfloat16 [2048, 2048], P(('seq', 'kvh'))
- value_gradient: bfloat16 [2048, 2048], P(('seq', 'kvh'))
The draws below stay inside these ranges and needn't reach their ends.
Inputs may be any that keep to these rules, and one draw needn't show every extreme that they name: `file_start`: entries never fall along the slab; each entry is at most its own token's position, and equals it at the first token of a file; the first file starts at 0 and the slab's last token begins a file of its own.
All inputs are finite; a program needn't handle non-finite values.
Results may differ from the reference program's by a relative error of at most 0.024.
Values may be sent and summed in bfloat16 or wider, within the bound.
A program may use at most 128 MiB of HBM per device.

```python
import math
import jax
import jax.numpy as jnp
from jax import lax

QUERY_HEADS = 32
KEY_VALUE_HEADS = 16
HEAD_SIZE = 128
WINDOW_TOKENS = 1024
SLAB_TOKENS = 2048


def file_starts(key):
    lengths = jax.random.randint(jax.random.fold_in(key, 11), (SLAB_TOKENS // 2 + 1,), 2, 3 * WINDOW_TOKENS + 1, dtype=jnp.int32)
    file_ends = jnp.cumsum(lengths).astype(jnp.int32)
    begins = file_ends - lengths
    positions = jnp.arange(SLAB_TOKENS, dtype=jnp.int32)
    file_index = jnp.searchsorted(file_ends, positions, side='right')
    starts = begins[file_index].astype(jnp.int32)
    return jnp.where(positions == SLAB_TOKENS - 1, positions, starts).astype(jnp.int32)


def drawn(key):
    starting_key = jax.random.fold_in(key, 5)
    query_key = jax.random.fold_in(starting_key, 1)
    key_random_seed = jax.random.fold_in(starting_key, 2)
    query_vals = jnp.clip(1.6 * jax.random.normal(query_key, (SLAB_TOKENS, QUERY_HEADS * HEAD_SIZE), jnp.float32), -8.0, 8.0)
    key_entries = jnp.clip(1.6 * jax.random.normal(key_random_seed, (SLAB_TOKENS, KEY_VALUE_HEADS * HEAD_SIZE), jnp.float32), -8.0, 8.0)
    return (query_vals, key_entries)


def draw_queries(key, part):
    return drawn(key)[0].astype(jnp.bfloat16)


def draw_keys(key, part):
    return drawn(key)[1].astype(jnp.bfloat16)


def draw_file_start(key, part):
    return file_starts(key)


def levels(key, dims, cuts, least, high):
    def one(dim, shards_of):
        steps = jax.random.uniform(jax.random.fold_in(jax.random.fold_in(key, 6), dim), (shards_of,), jnp.float32, least / len(cuts), high / len(cuts))
        return jnp.repeat(jnp.exp(steps), dims[dim] // shards_of).reshape((-1,) + (1,) * (len(dims) - dim - 1))

    level = one(*cuts[0])
    for cut in cuts[1:]:
        level = level * one(*cut)
    return level


def gaussian(stream_key, dims, scale, bound, cuts=(), held_as=jnp.bfloat16):
    result = jax.random.normal(stream_key, dims, jnp.float32) * scale
    if len(cuts) > 0:
        result = levels(stream_key, dims, cuts, -0.22, 0.18) * result
    return jnp.clip(result, min=-bound, max=bound).astype(held_as)


def setup_inputs(seed: int = 0) -> dict:
    key_of = jax.random.split(jax.random.key(seed), 6)
    return {
        "queries": draw_queries(jax.random.fold_in(key_of[5], 71), 0),
        "keys": draw_keys(jax.random.fold_in(key_of[5], 71), 0),
        "values": gaussian(key_of[2], (SLAB_TOKENS, KEY_VALUE_HEADS * HEAD_SIZE), 1.0, 6.0, ((0, 32),)),
        "out_grad": gaussian(key_of[3], (SLAB_TOKENS, QUERY_HEADS * HEAD_SIZE), 1.0, 6.0, ((0, 32),)),
        "file_start": draw_file_start(jax.random.fold_in(key_of[5], 71), 0),
    }


score_scale = 168.0 ** -0.5


def reference(queries, keys, values, out_grad, file_start):
    block_rows = math.gcd(SLAB_TOKENS, 512)
    key_extent = block_rows + WINDOW_TOKENS
    group_width = QUERY_HEADS // KEY_VALUE_HEADS
    leading_keys = jnp.concatenate([jnp.zeros((WINDOW_TOKENS, KEY_VALUE_HEADS * HEAD_SIZE), keys.dtype), keys], axis=0).reshape(WINDOW_TOKENS + SLAB_TOKENS, KEY_VALUE_HEADS, HEAD_SIZE)
    leading_values = jnp.concatenate([jnp.zeros((WINDOW_TOKENS, KEY_VALUE_HEADS * HEAD_SIZE), values.dtype), values], axis=0).reshape(WINDOW_TOKENS + SLAB_TOKENS, KEY_VALUE_HEADS, HEAD_SIZE)
    query_all = queries.reshape(SLAB_TOKENS, QUERY_HEADS, HEAD_SIZE)
    grad_all = out_grad.reshape(SLAB_TOKENS, QUERY_HEADS, HEAD_SIZE)
    span_offsets = jnp.arange(key_extent, dtype=jnp.int32)
    row_offsets = jnp.arange(block_rows, dtype=jnp.int32)

    def one_block(carry, block_index):
        key_running_sum, value_running_sum = carry
        start_row = (block_index * block_rows).astype(jnp.int32)
        query_block = lax.dynamic_slice_in_dim(query_all, start_row, block_rows, 0).astype(jnp.float32)
        grad_block = lax.dynamic_slice_in_dim(grad_all, start_row, block_rows, 0).astype(jnp.float32)
        key_window = lax.dynamic_slice_in_dim(leading_keys, start_row, key_extent, 0).astype(jnp.float32)
        value_window = lax.dynamic_slice_in_dim(leading_values, start_row, key_extent, 0).astype(jnp.float32)
        file_begins = lax.dynamic_slice_in_dim(file_start, start_row, block_rows, 0)
        query_pos = start_row + row_offsets
        key_pos = start_row - WINDOW_TOKENS + span_offsets
        lower_key = jnp.maximum(file_begins, query_pos - WINDOW_TOKENS + 1)
        allowed = (key_pos[None, :] >= lower_key[:, None]) & (key_pos[None, :] <= query_pos[:, None])
        key_rep = jnp.repeat(key_window, group_width, axis=1)
        value_rep = jnp.repeat(value_window, group_width, axis=1)
        scores = jnp.einsum("qhd,khd->hqk", query_block, key_rep) * score_scale
        scores = jnp.where(allowed[None], scores, -jnp.inf)
        row_peak = jnp.max(scores, axis=2, keepdims=True)
        log_total = row_peak + jnp.log(jnp.sum(jnp.exp(scores - row_peak), axis=2, keepdims=True))
        prob_full = jnp.exp(scores - log_total)
        prob_low = lax.optimization_barrier(prob_full.astype(jnp.bfloat16)).astype(jnp.float32)
        attention = jnp.einsum("hqk,khd->qhd", prob_low, value_rep).astype(jnp.bfloat16)
        row_delta = jnp.transpose(jnp.sum(grad_block * attention.astype(jnp.float32), axis=2))
        prob_grad = jnp.einsum("qhd,khd->hqk", grad_block, value_rep)
        score_grad = lax.optimization_barrier((prob_full * (prob_grad - row_delta[:, :, None])).astype(jnp.bfloat16)).astype(jnp.float32)
        query_grad = (score_scale * jnp.einsum("hqk,khd->qhd", score_grad, key_rep)).astype(jnp.bfloat16)
        key_portion = score_scale * jnp.einsum("hqk,qhd->khd", score_grad, query_block)
        key_portion = key_portion.reshape(key_extent, KEY_VALUE_HEADS, group_width, HEAD_SIZE).sum(axis=2)
        value_portion = jnp.einsum("hqk,qhd->khd", prob_low, grad_block)
        value_portion = value_portion.reshape(key_extent, KEY_VALUE_HEADS, group_width, HEAD_SIZE).sum(axis=2)
        key_running_sum = lax.dynamic_update_slice_in_dim(key_running_sum, lax.dynamic_slice_in_dim(key_running_sum, start_row, key_extent, 0) + key_portion, start_row, 0)
        value_running_sum = lax.dynamic_update_slice_in_dim(value_running_sum, lax.dynamic_slice_in_dim(value_running_sum, start_row, key_extent, 0) + value_portion, start_row, 0)
        return (key_running_sum, value_running_sum), (attention.reshape(block_rows, QUERY_HEADS * HEAD_SIZE), query_grad.reshape(block_rows, QUERY_HEADS * HEAD_SIZE))

    empty_running_sum = jnp.zeros((WINDOW_TOKENS + SLAB_TOKENS, KEY_VALUE_HEADS, HEAD_SIZE), jnp.float32)
    block_ids = jnp.arange(SLAB_TOKENS // block_rows, dtype=jnp.int32)
    (key_running_sum, value_running_sum), (attention, query_grad) = lax.scan(one_block, (empty_running_sum, empty_running_sum), block_ids)
    attn_out = attention.reshape(SLAB_TOKENS, QUERY_HEADS * HEAD_SIZE)
    query_grad = query_grad.reshape(SLAB_TOKENS, QUERY_HEADS * HEAD_SIZE)
    key_gradient = key_running_sum[WINDOW_TOKENS:].reshape(SLAB_TOKENS, KEY_VALUE_HEADS * HEAD_SIZE).astype(jnp.bfloat16)
    value_gradient = value_running_sum[WINDOW_TOKENS:].reshape(SLAB_TOKENS, KEY_VALUE_HEADS * HEAD_SIZE).astype(jnp.bfloat16)
    return (attn_out, query_grad, key_gradient, value_gradient)
```

```python
import functools
import math

import jax
import jax.numpy as jnp
from jax import lax
from jax.experimental import pallas as pl
from jax.experimental.pallas import tpu as pltpu
from jax.sharding import PartitionSpec as P

HEAD_SIZE = 128
WINDOW_TOKENS = 1024
SCALE = 168.0 ** (-0.5)
EXP2_SCALE = SCALE / math.log(2.0)
MASKED = -1e30
MESH = pl.DeviceIdType.MESH

NT = (((1,), (1,)), ((), ()))
NN = (((1,), (0,)), ((), ()))
TN = (((0,), (0,)), ((), ()))


def matmul(left, right, dims):
    return lax.dot_general(left, right, dims, preferred_element_type=jnp.float32)


def kernel(
    seq_count, kvh_count, kv_local, group, rows, reach,
    q_in, k_in, v_in, g_in, starts_ref,
    attn_out, dq_out, dk_out, dv_out,
    kv, qg, scores, out_t, dq_t, attn_buf, dq_buf, part, pair_send, pair_recv,
    chain_send, chain_recv, dkv_low,
    in_send, in_recv, in_local, out_send, out_recv, out_local,
    hop_send, mate_send, window_recv, back_pair_send, back_pair_recv,
    back_chain_send, back_chain_recv,
):
    depth = reach + reach % 2
    seq = lax.axis_index("seq")
    me = lax.axis_index("kvh")
    odd = lax.rem(seq, 2)
    mate = seq + 1 - 2 * odd
    piece = rows // kvh_count
    width = group * HEAD_SIZE
    has_next = seq + 2 < seq_count
    has_previous = seq >= 2

    barrier = pltpu.get_barrier_semaphore()
    for off in range(1, kvh_count):
        pl.semaphore_signal(
            barrier, inc=1, device_id=(seq, lax.rem(me + off, kvh_count)), device_id_type=MESH
        )
    pl.semaphore_signal(barrier, inc=1, device_id=(mate, me), device_id_type=MESH)

    @pl.when(has_next)
    def _():
        pl.semaphore_signal(barrier, inc=1, device_id=(seq + 2, me), device_id_type=MESH)

    @pl.when(has_previous)
    def _():
        pl.semaphore_signal(barrier, inc=1, device_id=(seq - 2, me), device_id_type=MESH)

    pl.semaphore_wait(
        barrier, kvh_count + has_next.astype(jnp.int32) + has_previous.astype(jnp.int32)
    )

    sources = (k_in, v_in, q_in, g_in)
    widths = (HEAD_SIZE, HEAD_SIZE, width, width)
    targets = (attn_out, dq_out, dk_out, dv_out)
    out_widths = (width, width, HEAD_SIZE, HEAD_SIZE)

    def in_source(kind, head, owner):
        start = pl.multiple_of((owner * kv_local + head) * widths[kind], 128)
        return sources[kind].at[:, pl.ds(start, widths[kind])]

    def in_target(kind, head):
        block = pl.ds(pl.multiple_of(me * piece, piece), piece)
        if kind < 2:
            return kv.at[0, head, kind, block, :]
        return qg.at[head, kind - 2, block, :]

    def in_copy(kind, head, off):
        peer = lax.rem(me + off, kvh_count)
        return pltpu.make_async_remote_copy(
            src_ref=in_source(kind, head, peer),
            dst_ref=in_target(kind, head),
            send_sem=in_send.at[kind, head, off - 1],
            recv_sem=in_recv.at[kind, head, off - 1],
            device_id=(seq, peer),
            device_id_type=MESH,
        )

    def in_own(kind, head):
        return pltpu.make_async_copy(
            in_source(kind, head, me), in_target(kind, head), in_local.at[kind, head]
        )

    def in_wait(kind, head):
        in_own(kind, head).wait()
        for off in range(1, kvh_count):
            in_copy(kind, head, off).wait_recv()

    def out_source(kind, head, owner):
        block = pl.ds(pl.multiple_of(owner * piece, piece), piece)
        if kind == 0:
            return attn_buf.at[head, block, :]
        if kind == 1:
            return dq_buf.at[head, block, :]
        return dkv_low.at[head, kind - 2, block, :]

    def out_target(kind, head):
        start = pl.multiple_of((me * kv_local + head) * out_widths[kind], 128)
        return targets[kind].at[:, pl.ds(start, out_widths[kind])]

    def out_copy(kind, head, off):
        peer = lax.rem(me + off, kvh_count)
        return pltpu.make_async_remote_copy(
            src_ref=out_source(kind, head, peer),
            dst_ref=out_target(kind, head),
            send_sem=out_send.at[kind, head, off - 1],
            recv_sem=out_recv.at[kind, head, off - 1],
            device_id=(seq, peer),
            device_id_type=MESH,
        )

    def out_own(kind, head):
        return pltpu.make_async_copy(
            out_source(kind, head, me), out_target(kind, head), out_local.at[kind, head]
        )

    def out_start(kind, head):
        for off in range(1, kvh_count):
            out_copy(kind, head, off).start()
        out_own(kind, head).start()

    def hop_copy(slot, head):
        return pltpu.make_async_remote_copy(
            src_ref=kv.at[slot, head],
            dst_ref=kv.at[slot + 2, head],
            send_sem=hop_send.at[slot // 2, head],
            recv_sem=window_recv.at[slot + 1, head],
            device_id=(seq + 2, me),
            device_id_type=MESH,
        )

    def mate_copy(slot, head):
        there = slot + 1 - 2 * odd
        return pltpu.make_async_remote_copy(
            src_ref=kv.at[slot, head],
            dst_ref=kv.at[there, head],
            send_sem=mate_send.at[slot // 2, head],
            recv_sem=window_recv.at[there - 1, head],
            device_id=(mate, me),
            device_id_type=MESH,
        )

    def arrived(slot, head):
        pltpu.make_async_remote_copy(
            src_ref=kv.at[slot, head],
            dst_ref=kv.at[slot, head],
            send_sem=hop_send.at[0, head],
            recv_sem=window_recv.at[slot - 1, head],
            device_id=(mate, me),
            device_id_type=MESH,
        ).wait_recv()

    def hops(slot):
        return jnp.logical_and(has_next, seq >= slot) if slot + 2 <= depth else None

    def mates(slot):
        if slot == 0:
            return odd == 0
        if slot + 1 <= reach:
            return seq >= slot
        return jnp.logical_and(odd == 1, seq >= slot)

    def send_on(slot, head):
        if hops(slot) is not None:
            @pl.when(hops(slot))
            def _():
                hop_copy(slot, head).start()

        @pl.when(mates(slot))
        def _():
            mate_copy(slot, head).start()

    def send_keys(head, carry):
        for kind in (0, 1):
            for off in range(1, kvh_count):
                in_copy(kind, head, off).start()
            in_own(kind, head).start()
        return carry

    def send_queries(head, carry):
        for kind in (2, 3):
            for off in range(1, kvh_count):
                in_copy(kind, head, off).start()
            in_own(kind, head).start()
        return carry

    lax.fori_loop(0, kv_local, send_keys, 0)
    lax.fori_loop(0, kv_local, send_queries, 0)

    def first_hop(head, carry):
        in_wait(0, head)
        in_wait(1, head)
        send_on(0, head)
        return carry

    lax.fori_loop(0, kv_local, first_hop, 0)

    for slot in range(2, depth, 2):

        def next_hop(head, carry, slot=slot):
            @pl.when(seq >= slot)
            def _():
                arrived(slot, head)

            send_on(slot, head)
            return carry

        lax.fori_loop(0, kv_local, next_hop, 0)

    row_pos = lax.broadcasted_iota(jnp.int32, (1, rows), 1)
    lower_row = jnp.maximum(starts_ref[...] - seq * rows, row_pos - (WINDOW_TOKENS - 1))
    lower = jnp.concatenate([lower_row] * group, axis=1)
    position = jnp.concatenate([row_pos] * group, axis=1)
    spots = lax.broadcasted_iota(jnp.int32, (rows, group * rows), 0)
    block_count = jnp.minimum(seq, reach) + 1

    def stacked(wide):
        return jnp.concatenate(
            [wide[:, i * HEAD_SIZE : (i + 1) * HEAD_SIZE] for i in range(group)], axis=0
        )

    def spread(tall):
        return jnp.concatenate([tall[i * rows : (i + 1) * rows] for i in range(group)], axis=1)

    def compute(head):
        queries = stacked(qg[head, 0])
        grads = stacked(qg[head, 1])

        def score_block(slot, peak):
            raw = matmul(kv[slot, head, 0], queries, NT)
            allowed = jnp.logical_and(
                spots >= lower + slot * rows, spots <= position + slot * rows
            )
            raw = jnp.where(allowed, raw, MASKED)
            scores[slot] = raw
            return jnp.maximum(peak, jnp.max(raw, axis=0, keepdims=True))

        peak = lax.fori_loop(
            0, block_count, score_block, jnp.full((1, group * rows), MASKED, jnp.float32)
        )
        out_t[...] = jnp.zeros_like(out_t)

        def value_block(slot, total):
            raised = jnp.exp2((scores[slot] - peak) * EXP2_SCALE)
            scores[slot] = raised
            out_t[...] += matmul(kv[slot, head, 1], raised.astype(jnp.bfloat16), TN)
            return total + jnp.sum(raised, axis=0, keepdims=True)

        total = lax.fori_loop(
            0, block_count, value_block, jnp.zeros((1, group * rows), jnp.float32)
        )
        inverse = 1.0 / total
        attention = (out_t[...] * inverse).astype(jnp.bfloat16).astype(jnp.float32)
        attn_buf[head] = spread(jnp.transpose(attention).astype(jnp.bfloat16))
        out_start(0, head)
        delta = jnp.sum(
            jnp.transpose(grads.astype(jnp.float32)) * attention, axis=0, keepdims=True
        )
        dq_t[...] = jnp.zeros_like(dq_t)

        def grad_block(slot):
            probs = scores[slot] * inverse
            value_part = matmul(probs.astype(jnp.bfloat16), grads, NN)
            prob_grad = matmul(kv[slot, head, 1], grads, NT)
            score_grad = (probs * (prob_grad - delta)).astype(jnp.bfloat16)
            key_part = matmul(score_grad, queries, NN) * SCALE
            dq_t[...] += matmul(kv[slot, head, 0], score_grad, TN)
            return key_part, value_part

        for slot in range(reach + 1):

            @pl.when(seq >= slot)
            def _(slot=slot):
                key_part, value_part = grad_block(slot)
                if slot % 2:
                    pair_send[slot // 2, head, 0] = key_part.astype(jnp.bfloat16)
                    pair_send[slot // 2, head, 1] = value_part.astype(jnp.bfloat16)
                    back_pair(slot, head).start()
                else:
                    part[slot // 2, head, 0] = key_part
                    part[slot // 2, head, 1] = value_part

        if depth > reach:
            part[depth // 2, head] = jnp.zeros_like(part[depth // 2, head])

        dq_buf[head] = spread(jnp.transpose(dq_t[...] * SCALE).astype(jnp.bfloat16))
        out_start(1, head)

    def back_pair(slot, head):
        there = slot // 2 + (1 - odd)
        return pltpu.make_async_remote_copy(
            src_ref=pair_send.at[slot // 2, head],
            dst_ref=pair_recv.at[there, head],
            send_sem=back_pair_send.at[slot // 2, head],
            recv_sem=back_pair_recv.at[there, head],
            device_id=(mate, me),
            device_id_type=MESH,
        )

    def back_chain(slot, head):
        return pltpu.make_async_remote_copy(
            src_ref=chain_send.at[slot // 2 - 1, head],
            dst_ref=chain_recv.at[slot // 2 - 1, head],
            send_sem=back_chain_send.at[slot // 2 - 1, head],
            recv_sem=back_chain_recv.at[slot // 2 - 1, head],
            device_id=(seq - 2, me),
            device_id_type=MESH,
        )

    def collect(slot, head):
        half = slot // 2

        @pl.when(mates(slot))
        def _():
            pltpu.make_async_remote_copy(
                src_ref=pair_recv.at[half, head],
                dst_ref=pair_recv.at[half, head],
                send_sem=back_pair_send.at[0, head],
                recv_sem=back_pair_recv.at[half, head],
                device_id=(mate, me),
                device_id_type=MESH,
            ).wait_recv()
            part[half, head] += pair_recv[half, head].astype(jnp.float32)

        if slot + 2 <= depth:

            @pl.when(hops(slot))
            def _():
                pltpu.make_async_remote_copy(
                    src_ref=chain_recv.at[half, head],
                    dst_ref=chain_recv.at[half, head],
                    send_sem=back_chain_send.at[half, head],
                    recv_sem=back_chain_recv.at[half, head],
                    device_id=(mate, me),
                    device_id_type=MESH,
                ).wait_recv()
                part[half, head] += chain_recv[half, head].astype(jnp.float32)

        if slot == 0:
            dkv_low[head] = part[0, head].astype(jnp.bfloat16)
            out_start(2, head)
            out_start(3, head)
        else:

            @pl.when(seq >= slot)
            def _():
                chain_send[half - 1, head] = part[half, head].astype(jnp.bfloat16)
                back_chain(slot, head).start()

    levels = depth // 2 + 1

    def step(turn, carry):
        @pl.when(turn < kv_local)
        def _():
            head = turn

            @pl.when(seq >= depth)
            def _():
                arrived(depth, head)

            send_on(depth, head)
            for slot in range(1, reach + 1, 2):

                @pl.when(seq >= slot)
                def _(slot=slot):
                    arrived(slot, head)

            in_wait(2, head)
            in_wait(3, head)
            compute(head)

        for level in range(levels):
            lag = level + 1

            @pl.when(jnp.logical_and(turn >= lag, turn < kv_local + lag))
            def _(level=level, lag=lag):
                collect(depth - 2 * level, turn - lag)

        return carry

    lax.fori_loop(0, kv_local + levels, step, 0)

    def finish(head, carry):
        for kind in range(4):
            out_own(kind, head).wait()
            for off in range(1, kvh_count):
                in_copy(kind, head, off).wait_send()
                out_copy(kind, head, off).wait()
        for slot in range(0, depth + 1, 2):
            if slot + 2 <= depth:

                @pl.when(hops(slot))
                def _(slot=slot):
                    hop_copy(slot, head).wait_send()

            @pl.when(mates(slot))
            def _(slot=slot):
                mate_copy(slot, head).wait_send()

            if slot > 0:

                @pl.when(seq >= slot)
                def _(slot=slot):
                    back_chain(slot, head).wait_send()

        for slot in range(1, reach + 1, 2):

            @pl.when(seq >= slot)
            def _(slot=slot):
                back_pair(slot, head).wait_send()

        return carry

    lax.fori_loop(0, kv_local, finish, 0)


def body(seq_count, kvh_count, queries, keys, values, out_grad, file_start):
    rows = file_start.shape[0]
    kv_local = keys.shape[1] // (HEAD_SIZE * kvh_count)
    group = queries.shape[1] // keys.shape[1]
    reach = (WINDOW_TOKENS + rows - 1) // rows
    depth = reach + reach % 2
    half = depth // 2
    bf16, f32 = jnp.bfloat16, jnp.float32
    block = (kv_local, 2, rows, HEAD_SIZE)
    width = group * HEAD_SIZE
    dma = pltpu.SemaphoreType.DMA
    vmem = pl.BlockSpec(memory_space=pltpu.VMEM)
    return pl.pallas_call(
        functools.partial(kernel, seq_count, kvh_count, kv_local, group, rows, reach),
        out_shape=tuple(
            jax.ShapeDtypeStruct(like.shape, bf16) for like in (queries, queries, keys, values)
        ),
        in_specs=[vmem] * 5,
        out_specs=(vmem,) * 4,
        scratch_shapes=[
            pltpu.VMEM((depth + 1, *block), bf16),
            pltpu.VMEM((kv_local, 2, rows, width), bf16),
            pltpu.VMEM((reach + 1, rows, group * rows), f32),
            pltpu.VMEM((HEAD_SIZE, group * rows), f32),
            pltpu.VMEM((HEAD_SIZE, group * rows), f32),
            pltpu.VMEM((kv_local, rows, width), bf16),
            pltpu.VMEM((kv_local, rows, width), bf16),
            pltpu.VMEM((half + 1, *block), f32),
            pltpu.VMEM((half, *block), bf16),
            pltpu.VMEM((half + 1, *block), bf16),
            pltpu.VMEM((half, *block), bf16),
            pltpu.VMEM((half, *block), bf16),
            pltpu.VMEM(block, bf16),
            dma((4, kv_local, kvh_count - 1)),
            dma((4, kv_local, kvh_count - 1)),
            dma((4, kv_local)),
            dma((4, kv_local, kvh_count - 1)),
            dma((4, kv_local, kvh_count - 1)),
            dma((4, kv_local)),
            dma((half, kv_local)),
            dma((half + 1, kv_local)),
            dma((depth, kv_local)),
            dma((half, kv_local)),
            dma((half + 1, kv_local)),
            dma((half, kv_local)),
            dma((half, kv_local)),
        ],
        compiler_params=pltpu.CompilerParams(
            collective_id=0, has_side_effects=True, vmem_limit_bytes=56 * 1024 * 1024
        ),
    )(queries, keys, values, out_grad, file_start.reshape(1, rows))


def solution(mesh):
    token_spec = P(("seq", "kvh"), None)
    return jax.shard_map(
        functools.partial(body, mesh.shape["seq"], mesh.shape["kvh"]),
        mesh=mesh,
        in_specs=(token_spec,) * 4 + (P("seq"),),
        out_specs=(token_spec,) * 4,
        check_vma=False,
    )
```
